32 devices in a mesh: node: 4 (over y, x), wide: 8 (over z, core).
Axes of the slice: x: 2, y: 2, z: 4, core: 2. Of those that a mesh axis runs over, the one named last changes fastest.
Arguments:
- feats: bfloat16 [8192, 40], P(('node', 'wide')), may hold values from -6 to 6
- utt_lengths: int32 [32, 8], P(('node', 'wide')), may hold values from 1 to 128, 256 in all within a row
- frame_mask: int32 [8192], P(('node', 'wide')), may hold values from 0 to 1, as said below
- targets: int32 [8192], P(('node', 'wide')), may hold values from 0 to 9303
- val_feats: bfloat16 [4096, 40], P(('node', 'wide')), may hold values from -6 to 6
- val_mask: int32 [4096], P(('node', 'wide')), may hold values from 0 to 1, as said below
- val_targets: int32 [4096], P(('node', 'wide')), may hold values from 0 to 9303
- master: float32 [47200, 512], P(('node', 'wide')), as said below
- first_moment: float32 [47200, 512], P(('node', 'wide')), may hold values from -0.0012207031 to 0.0012207031
- second_moment: float32 [47200, 512], P(('node', 'wide')), may hold values from 8.275953e-09 to 8.2759534e-08
- residual: float32 [377600, 512], P(('node', 'wide')), as said below
- average: float32 [47200, 512], P(('node', 'wide')), as said below
Outputs:
- loss: float32 [], replicated
- val_loss: float32 [], replicated
- grad_norm: float32 [], replicated
- master_new: float32 [47200, 512], P(('node', 'wide'))
- first_new: float32 [47200, 512], P(('node', 'wide'))
- second_new: float32 [47200, 512], P(('node', 'wide'))
- residual_new: float32 [377600, 512], P(('node', 'wide'))
- average_new: float32 [47200, 512], P(('node', 'wide'))
The draws below stay inside these ranges and needn't reach their ends.
Inputs may be any that keep to these rules, and one draw needn't show every extreme that they name: `frame_mask`: the first frame of every device counts; the share of counted frames rises over the devices in order from about a quarter to all. `val_mask`: the first validation frame of every device counts; the share of counted frames rises over the devices in order from about a quarter to all. `utt_lengths`: each row fills the device's 256 frames. `master`: parameters of order of their layer's usual scale. `average`: like master. `residual`: real values of either sign.
All inputs are finite; a program needn't handle non-finite values.
Results may differ from the reference program's by a relative error of at most 0.0003.
The reference program's roundings to bfloat16 on the way count: a program that leaves them out, or rounds other values in their place, can miss the bound.
Values may be sent and summed in bfloat16 or wider, within the bound.
No kernel may reach another device: no remote copies, remote signals or barrier semaphores. Data moves between devices by JAX's collectives and lax.ppermute only.
A program may use at most 640 MiB of HBM per device.

```python
import math
import jax
import jax.numpy as jnp
import numpy as np
from jax import lax

MEL = 40
CONTEXT = 11
UNITS = 2048
SENONES = 9304
D_IN = 440
TOK_DEV = 256
UTTS = 8
LONGEST = 128
VAL_DEV = 128
WID = 512
STEP_COUNT = 8
TOKENS = 8192
VAL_TOKENS = 4096
PARAMS = 24163416
ROWS = 47200
QROWS = 11800
SROWS = 1475
N_NODE = 4
N_WIDE = 8
DEVICES = 32


def scale_table(index):
    end_in = D_IN * UNITS
    end_bias_in = end_in + UNITS
    end_mid = end_bias_in + UNITS * UNITS
    end_bias_mid = end_mid + UNITS
    end_out = end_bias_mid + UNITS * SENONES
    return jnp.where(index < end_in, 2.0 / math.sqrt(D_IN), jnp.where(index < end_bias_in, 0.5, jnp.where(index < end_mid, 2.0 / math.sqrt(UNITS), jnp.where(index < end_bias_mid, 0.5, jnp.where(index < end_out, 3.0 / math.sqrt(UNITS), jnp.where(index < PARAMS, 0.5, 0.05))))))


def parameter_draw(key):
    index = jnp.arange(ROWS * WID, dtype=jnp.int32).reshape(ROWS, WID)
    noise = jnp.clip(jax.random.normal(key, (ROWS, WID), jnp.float32), -4.0, 4.0)
    return noise * scale_table(index)


def draw_master(key, part):
    return parameter_draw(jax.random.fold_in(key, 11))


def draw_average(key, part):
    return parameter_draw(jax.random.fold_in(key, 12))


def draw_residual(key, part):
    devices = N_NODE * N_WIDE
    base = 0.94 * TOKENS / math.sqrt(N_WIDE * ROWS * WID)
    noise = jnp.clip(jax.random.normal(jax.random.fold_in(key, 13), (devices * QROWS, WID), jnp.float32), -4.0, 4.0)
    where_r = jnp.arange(devices * QROWS, dtype=jnp.int32)
    owner = where_r // QROWS
    buffer_row = owner // N_WIDE * QROWS + where_r % QROWS
    ramp = 1.0 + 2.0 * buffer_row.astype(jnp.float32) / ROWS
    return noise * (base * ramp)[:, None]


def counted_frames(key, length):
    devices = N_NODE * N_WIDE
    ramp = 64 + 192 * jnp.arange(devices, dtype=jnp.int32) // max(devices - 1, 1)
    jitter = jax.random.randint(jax.random.fold_in(key, 1), (devices,), -8, 9)
    level = jnp.clip(ramp + jitter, 64, 256)
    draw = jax.random.randint(jax.random.fold_in(key, 2), (devices, length), 0, 256)
    first = jnp.arange(length, dtype=jnp.int32)[None, :] == 0
    live = (draw < level[:, None]) | first
    return live.astype(jnp.int32).reshape(-1)


def draw_frame_mask(key, part):
    return counted_frames(jax.random.fold_in(key, 21), TOK_DEV)


def draw_val_mask(key, part):
    return counted_frames(jax.random.fold_in(key, 22), VAL_DEV)


def touch_ends(drawn, key, low, top_value):
    longest = drawn.shape.index(max(drawn.shape))
    spots = []
    for shift in (0, 1):
        where = [jax.random.randint(jax.random.fold_in(key, axis), (), 0, length) for axis, length in enumerate(drawn.shape)]
        where[longest] = (where[longest] + shift) % drawn.shape[longest]
        spots.append(tuple(where))
    return drawn.at[spots[0]].set(low).at[spots[1]].set(top_value)


def levels(key, extent, cuts, smallest, top_value):
    def one(dim, shards_of):
        heights = jax.random.uniform(jax.random.fold_in(jax.random.fold_in(key, 6), dim), (shards_of,), jnp.float32, smallest / len(cuts), top_value / len(cuts))
        return jnp.repeat(jnp.exp(heights), extent[dim] // shards_of).reshape((-1,) + (1,) * (len(extent) - dim - 1))

    loudness = one(*cuts[0])
    for cut in cuts[1:]:
        loudness = loudness * one(*cut)
    return loudness


def rank_bounds(amount, lean):
    loads = [(1 << 20) // math.isqrt(grade ** lean) + 1 for grade in range(1, amount + 1)]
    scale = 1 + sum(loads) // (1 << 30)
    return np.cumsum(np.array([max(1, weight // scale) for weight in loads]))


def skewed_ids(stream_key, extent, amount, skew):
    listing = rank_bounds(amount, skew)
    lot = jax.random.randint(jax.random.fold_in(stream_key, 1), extent, 0, int(listing[amount - 1]))
    rank = jnp.searchsorted(jnp.asarray(listing, jnp.int32), lot, side="right")
    return jax.random.permutation(jax.random.fold_in(stream_key, 2), amount)[rank].astype(jnp.int32)


def length_profile(amount, total, most, slope):
    portions = [(1 << 20) // math.isqrt(grade ** slope) + 1 for grade in range(2, amount + 1)]
    spare, given = total - most - (amount - 1), [1] * (amount - 1)
    while spare > 0:
        movable = [i for i in range(amount - 1) if given[i] < most]
        whole, left = sum([portions[i] for i in movable]), spare
        for i in movable:
            more = min(most - given[i], max(1, left * portions[i] // whole), spare)
            given[i] = given[i] + more
            spare = spare - more
    return np.array([most] + given)


def uneven(key, number_of, total, bound, skew):
    if number_of == 2:
        one = jax.random.randint(key, (), max(1, total - bound), min(bound, total - 1) + 1)
        return jnp.stack([one, total - one])
    sizes = jnp.asarray(length_profile(number_of, total, bound, skew), jnp.int32)
    twos = (number_of - 1) // 2
    giver, receiver = sizes[1:1 + 2 * twos:2], sizes[2:2 + 2 * twos:2]
    margin = jnp.minimum(giver - 1, bound - receiver)
    passed = jax.random.randint(jax.random.fold_in(key, 1), (twos,), 0, 1 << 20) % (margin + 1)
    sizes = sizes.at[1:1 + 2 * twos:2].set(giver - passed).at[2:2 + 2 * twos:2].set(receiver + passed)
    return sizes[jax.random.permutation(jax.random.fold_in(key, 2), number_of)]


def centred(key, shape, scale, limit, split=(), kind=jnp.bfloat16):
    result = scale * jax.random.normal(key, shape, jnp.float32)
    if split:
        result = result * levels(key, shape, split, -0.22, 0.18)
    return jnp.clip(result, -limit, limit).astype(kind)


def setup_inputs(seed: int = 0) -> dict:
    seeds = jax.random.split(jax.random.key(seed), 13)
    feats = centred(seeds[0], (TOKENS, MEL), 1.0, 6.0, ((0, 32),))
    utt_lengths = jax.vmap(lambda own: uneven(own, UTTS, TOK_DEV, LONGEST, 2))(jax.random.split(seeds[1], DEVICES)).reshape((DEVICES, UTTS)).astype(jnp.int32)
    frame_mask = draw_frame_mask(jax.random.fold_in(seeds[12], 71), 0)
    targets = touch_ends(skewed_ids(seeds[3], (TOKENS,), SENONES, 2), jax.random.fold_in(seeds[3], 3), 0, SENONES - 1).astype(jnp.int32)
    val_feats = centred(seeds[4], (VAL_TOKENS, MEL), 1.0, 6.0, ((0, 32),))
    val_mask = draw_val_mask(jax.random.fold_in(seeds[12], 71), 0)
    val_targets = touch_ends(skewed_ids(seeds[6], (VAL_TOKENS,), SENONES, 2), jax.random.fold_in(seeds[6], 3), 0, SENONES - 1).astype(jnp.int32)
    master = draw_master(jax.random.fold_in(seeds[12], 71), 0)
    first_moment = centred(seeds[8], (ROWS, WID), (ROWS * WID) ** -0.5, 0.0012207031, ((0, 32),), jnp.float32)
    second_moment = jnp.clip(jnp.exp(math.log(8.275953433667382e-08) - 2.3025851 * jax.random.uniform(seeds[9], (ROWS, WID), jnp.float32) ** levels(seeds[9], (ROWS, WID), ((0, 32),), -0.2, 0.2)), 8.275953256031698e-09, 8.275953433667382e-08)
    residual = draw_residual(jax.random.fold_in(seeds[12], 71), 0)
    average = draw_average(jax.random.fold_in(seeds[12], 71), 0)
    return dict(feats=feats, utt_lengths=utt_lengths, frame_mask=frame_mask, targets=targets, val_feats=val_feats, val_mask=val_mask, val_targets=val_targets, master=master, first_moment=first_moment, second_moment=second_moment, residual=residual, average=average)


@jax.custom_vjp
def low(v):
    return lax.optimization_barrier(v.astype(jnp.bfloat16)).astype(jnp.float32)

@jax.custom_vjp
def low_back(v):
    return v

def low_keep(v):
    return (low(v), None)

def low_pass(kept, grad):
    return (grad,)

def back_keep(v):
    return (v, None)

def back_low(kept, grad):
    return (low(grad),)
low.defvjp(low_keep, low_pass)
low_back.defvjp(back_keep, back_low)
CLIP_NORM = 1.0
LEARN_RATE = 0.02
BETA_ONE = 0.5
BETA_TWO = 0.5
DECAY = 0.1
AVG_KEEP = 0.9
EPS_ADAM = 1e-08
HIGH = lax.Precision.HIGHEST

def stack_frames(feats, lengths):
    count = feats.shape[0]
    ends = jnp.cumsum(lengths).astype(jnp.int32)
    starts = (ends - lengths).astype(jnp.int32)
    where_t = jnp.arange(count, dtype=jnp.int32)[:, None]
    inside = (where_t >= starts[None, :]) & (where_t < ends[None, :])
    first = lax.optimization_barrier(jnp.sum(jnp.where(inside, starts[None, :], 0), axis=1)).astype(jnp.int32)
    last = (lax.optimization_barrier(jnp.sum(jnp.where(inside, ends[None, :], 0), axis=1)) - 1).astype(jnp.int32)
    offsets = jnp.arange(CONTEXT, dtype=jnp.int32) - CONTEXT // 2
    index = jnp.clip(where_t + offsets[None, :], first[:, None], last[:, None]).astype(jnp.int32)
    return feats[index].reshape(count, CONTEXT * feats.shape[1])

def unpack(flat):
    line = flat.reshape(-1)
    shapes = [(D_IN, UNITS), (UNITS,), (UNITS, UNITS), (UNITS,), (UNITS, SENONES), (SENONES,)]
    pieces = []
    start = 0
    for shape in shapes:
        length = math.prod(shape)
        pieces.append(line[start:start + length].reshape(shape))
        start = start + length
    return tuple(pieces)

def product(left, right):
    return jnp.dot(left, right, precision=HIGH, preferred_element_type=jnp.float32)

def frame_ce(params, stacked, labels):
    w_in, b_in, w_mid, b_mid, w_out, b_out = params
    h_one = low(jax.nn.sigmoid(low_back(product(stacked, w_in) + b_in)))
    h_two = low(jax.nn.sigmoid(low_back(product(h_one, w_mid) + b_mid)))
    logits = low_back(product(h_two, w_out) + b_out)
    picked = jnp.take_along_axis(logits, labels[:, None], axis=1)[:, 0]
    return jax.nn.logsumexp(logits, axis=1) - picked

def reference(feats, utt_lengths, frame_mask, targets, val_feats, val_mask, val_targets, master, first_moment, second_moment, residual, average):
    devices = N_NODE * N_WIDE
    stacked = jax.vmap(stack_frames)(feats.reshape(devices, TOK_DEV, MEL), utt_lengths)
    stacked = stacked.astype(jnp.float32).reshape(N_NODE, N_WIDE, TOK_DEV, D_IN)
    labels = targets.reshape(N_NODE, N_WIDE, TOK_DEV)
    weights = frame_mask.astype(jnp.float32).reshape(N_NODE, N_WIDE, TOK_DEV)
    params = tuple((low(piece) for piece in unpack(master)))
    carried = residual.reshape(N_NODE, N_WIDE, QROWS, WID)

    def one_wide(state, wide):
        decoded, loss_acc = state
        inputs = lax.dynamic_index_in_dim(stacked, wide, 1, keepdims=False).reshape(N_NODE * TOK_DEV, D_IN)
        marks = lax.dynamic_index_in_dim(labels, wide, 1, keepdims=False).reshape(-1)
        scaled = lax.dynamic_index_in_dim(weights, wide, 1, keepdims=False).reshape(-1)

        def summed(values):
            return jnp.sum(scaled * frame_ce(values, inputs, marks))
        loss_part, pullback = jax.vjp(summed, params)
        grads = pullback(jnp.ones_like(loss_part))[0]
        flat = jnp.concatenate([piece.reshape(-1) for piece in grads] + [jnp.zeros((ROWS * WID - PARAMS,), jnp.float32)])
        flat = flat.reshape(N_NODE, QROWS, WID)
        rest = lax.dynamic_index_in_dim(carried, wide, 1, keepdims=False)
        values = flat + rest
        signs = jnp.where(rest >= 0, 1.0, -1.0).astype(jnp.float32)
        blocks = (signs * values).reshape(N_NODE, N_WIDE, SROWS, WID)
        scales = lax.optimization_barrier(jnp.mean(blocks, axis=2, keepdims=True))
        coded = (signs.reshape(N_NODE, N_WIDE, SROWS, WID) * scales).reshape(N_NODE, QROWS, WID)
        return ((decoded + coded, loss_acc + loss_part), values - coded)
    start = (jnp.zeros((N_NODE, QROWS, WID), jnp.float32), jnp.zeros((), jnp.float32))
    (decoded, loss_sum), kept = lax.scan(one_wide, start, jnp.arange(N_WIDE, dtype=jnp.int32))
    residual_new = jnp.transpose(kept, (1, 0, 2, 3)).reshape(devices * QROWS, WID)
    decoded = decoded.reshape(ROWS, WID)
    count = jnp.sum(frame_mask.astype(jnp.float32))
    loss = loss_sum / count
    grad_norm = jnp.sqrt(jnp.sum(decoded * decoded)) / count
    factor = jnp.minimum(1.0, CLIP_NORM / (grad_norm + 1e-06))
    grad = decoded * (factor / count)
    first_new = BETA_ONE * first_moment + (1.0 - BETA_ONE) * grad
    second_new = BETA_TWO * second_moment + (1.0 - BETA_TWO) * grad * grad
    first_hat = first_new / (1.0 - BETA_ONE ** STEP_COUNT)
    second_hat = second_new / (1.0 - BETA_TWO ** STEP_COUNT)
    master_new = master - LEARN_RATE * (first_hat / (jnp.sqrt(second_hat) + EPS_ADAM) + DECAY * master)
    average_new = AVG_KEEP * average + (1.0 - AVG_KEEP) * master_new
    val_params = tuple((low(piece) for piece in unpack(average_new)))
    single = jnp.full((devices, 1), VAL_DEV, jnp.int32)
    val_stacked = jax.vmap(stack_frames)(val_feats.reshape(devices, VAL_DEV, MEL), single)
    val_stacked = val_stacked.astype(jnp.float32).reshape(devices * VAL_DEV, D_IN)
    val_weights = val_mask.astype(jnp.float32)
    val_ce = frame_ce(val_params, val_stacked, val_targets)
    val_loss = jnp.sum(val_weights * val_ce) / jnp.sum(val_weights)
    return (loss, val_loss, grad_norm, master_new, first_new, second_new, residual_new, average_new)
```

```python
import functools

import jax
import jax.numpy as jnp
from jax import lax
from jax.experimental import pallas as pl
from jax.experimental.pallas import tpu as pltpu
from jax.sharding import PartitionSpec as P

CONTEXT = 11
UNITS = 2048
SENONES = 9304
D_IN = 440
STEP_COUNT = 8
LANES = 128
PERIOD = 16
PERIOD_GROUPS = PERIOD * SENONES // LANES
TILES = -(-SENONES // LANES)
HEAD_ROWS = D_IN + 1 + UNITS + 1
HEAD_GROUPS = HEAD_ROWS * UNITS // LANES
TURN_TILES = 80
BLOCK = 104

CLIP_NORM = 1.0
LEARN_RATE = 0.02
BETA_ONE = 0.5
BETA_TWO = 0.5
DECAY = 0.1
AVG_KEEP = 0.9
EPS_ADAM = 1e-08


def stack_frames(feats, lengths):
    count = feats.shape[0]
    ends = jnp.cumsum(lengths)
    starts = ends - lengths
    where_t = jnp.arange(count, dtype=jnp.int32)[:, None]
    inside = (where_t >= starts[None, :]) & (where_t < ends[None, :])
    first = jnp.sum(jnp.where(inside, starts[None, :], 0), axis=1)
    last = jnp.sum(jnp.where(inside, ends[None, :], 0), axis=1) - 1
    offsets = jnp.arange(CONTEXT, dtype=jnp.int32) - CONTEXT // 2
    index = jnp.clip(where_t + offsets[None, :], first[:, None], last[:, None])
    return feats[index].reshape(count, CONTEXT * feats.shape[1])


def tile_width(tile):
    return min(LANES, SENONES - tile * LANES)


def unfold_kernel(flat_ref, out_ref, wide_ref, turn_ref):
    groups = flat_ref.shape[0]
    steps = groups // LANES

    def widen(step, carry):
        at = pl.multiple_of(step * LANES, LANES)
        wide_ref[pl.ds(at, LANES), :] = flat_ref[pl.ds(at, LANES), :].astype(jnp.float32)
        return carry

    lax.fori_loop(0, steps, widen, 0)
    tail = groups - steps * LANES
    if tail:
        wide_ref[pl.ds(steps * LANES, tail), :] = flat_ref[pl.ds(steps * LANES, tail), :].astype(jnp.float32)
    lane = lax.broadcasted_iota(jnp.int32, (TURN_TILES, LANES), 1)

    def period(step, carry):
        base = step * PERIOD_GROUPS
        for i in range(PERIOD):
            group, shift = divmod(SENONES * i, LANES)
            value = wide_ref[pl.ds(base + group, TURN_TILES), :]
            if shift:
                following = wide_ref[pl.ds(base + group + 1, TURN_TILES), :]
                value = pltpu.roll(jnp.where(lane >= shift, value, following), LANES - shift, 1)
            turn_ref[pl.ds(i, TURN_TILES, stride=PERIOD), :] = value
        rows = pl.ds(pl.multiple_of(step * PERIOD, PERIOD), PERIOD)
        for tile in range(TILES):
            width = tile_width(tile)
            piece = turn_ref[pl.ds(tile * PERIOD, PERIOD), :].astype(jnp.bfloat16)
            out_ref[rows, pl.ds(tile * LANES, width)] = piece[:, :width]
        return carry

    lax.fori_loop(0, out_ref.shape[0] // PERIOD, period, 0)


def unfold(flat):
    span = PERIOD * PERIOD
    groups = PERIOD * PERIOD_GROUPS
    return pl.pallas_call(
        unfold_kernel,
        grid=(UNITS // span,),
        out_shape=jax.ShapeDtypeStruct((UNITS, SENONES), jnp.bfloat16),
        in_specs=[
            pl.BlockSpec((pl.Element(groups), pl.Element(LANES)), lambda m: (PERIOD * (HEAD_GROUPS // PERIOD + PERIOD_GROUPS * m), 0))
        ],
        out_specs=pl.BlockSpec((span, SENONES), lambda m: (m, 0)),
        scratch_shapes=[
            pltpu.VMEM((groups + TURN_TILES + 16, LANES), jnp.float32),
            pltpu.VMEM((TURN_TILES * PERIOD, LANES), jnp.float32),
        ],
    )(flat)


def unpack(flat):
    head = flat[:HEAD_GROUPS].reshape(HEAD_ROWS, UNITS)
    w_in = head[:D_IN]
    b_in = head[D_IN]
    w_mid = head[D_IN + 1 : D_IN + 1 + UNITS]
    b_mid = head[D_IN + 1 + UNITS]
    at = HEAD_GROUPS + UNITS * SENONES // LANES
    b_out = flat[at : at + TILES].reshape(-1)[:SENONES]
    return (w_in, b_in, w_mid, b_mid, unfold(flat), b_out)


def gather_flat(block):
    rows = block.shape[0] * block.shape[1] // LANES
    low = block.astype(jnp.bfloat16).reshape(rows, LANES)
    return lax.all_gather(low, ("node", "wide"), axis=0, tiled=True)


def layer_forward(inputs, weight, bias):
    return jnp.dot(inputs, weight, preferred_element_type=jnp.float32) + bias.astype(jnp.float32)


def contract_rows(left, right):
    return lax.dot_general(left, right, (((0,), (0,)), ((), ())), preferred_element_type=jnp.float32)


def contract_columns(left, right):
    return lax.dot_general(left, right, (((1,), (1,)), ((), ())), preferred_element_type=jnp.float32)


def run_layers(params, stacked):
    w_in, b_in, w_mid, b_mid, w_out, b_out = params
    sig_one = jax.nn.sigmoid(layer_forward(stacked, w_in, b_in))
    h_one = sig_one.astype(jnp.bfloat16)
    sig_two = jax.nn.sigmoid(layer_forward(h_one, w_mid, b_mid))
    h_two = sig_two.astype(jnp.bfloat16)
    logits = layer_forward(h_two, w_out, b_out)
    return (sig_one, h_one, sig_two, h_two, logits)


def frame_terms(logits, labels, weights):
    hit = labels[:, None] == lax.broadcasted_iota(jnp.int32, logits.shape, 1)
    top = jnp.max(logits, axis=1)
    total = jnp.sum(jnp.exp(logits - top[:, None]), axis=1)
    picked = jnp.sum(jnp.where(hit, logits, 0.0), axis=1)
    lse = jnp.log(total) + top
    return (jnp.sum(weights * (lse - picked)), lse, hit)


def pack_signs(rest):
    bits = (rest >= 0).astype(jnp.int32).reshape(rest.shape[0], rest.shape[1] // 32, 32)
    shifts = jnp.arange(32, dtype=jnp.int32)
    return jnp.sum(jnp.left_shift(bits, shifts), axis=2)


def unpack_signs(words):
    shifts = jnp.arange(32, dtype=jnp.int32)
    bits = jnp.bitwise_and(jnp.right_shift(words[..., None], shifts), 1)
    signs = (2 * bits - 1).astype(jnp.float32)
    return signs.reshape(words.shape[:-1] + (words.shape[-1] * 32,))


def padded(values, columns):
    count = values.shape[0]
    one = jnp.ones((count, 1), jnp.bfloat16)
    rest = jnp.zeros((count, columns - values.shape[1] - 1), jnp.bfloat16)
    return jnp.concatenate([values, one, rest], axis=1)


def code_kernel(plan, offset_ref, *refs):
    grad_refs = refs[: plan["inputs"]]
    residual_ref, new_ref, scale_ref, flat_ref, turn_ref, sum_ref = refs[plan["inputs"] :]
    step = pl.program_id(0)
    head, body, chunks = plan["head"], plan["body"], plan["chunks"]
    chunk, shard, margin, overlap = plan["chunk"], plan["shard"], plan["margin"], plan["overlap"]
    count = sum_ref.shape[0] // 8
    per_row = residual_ref.shape[1] // LANES
    if head:

        def place(ref, row):
            for tile in range(UNITS // LANES):
                at = row * (UNITS // LANES) + tile
                flat_ref[pl.ds(at, BLOCK, stride=UNITS // LANES), :] = ref[:, pl.ds(tile * LANES, LANES)]

        split = plan["split"]

        @pl.when(step < split)
        def _():
            place(grad_refs[0], step * BLOCK)

        @pl.when((step >= split) & (step < head))
        def _():
            place(grad_refs[1], D_IN + 1 + (step - split) * BLOCK)

    out_grad = grad_refs[-1]

    @pl.when((step >= head) & (step < head + body))
    def _():
        base = offset_ref[0] + (step - head) * PERIOD_GROUPS
        for tile in range(TILES):
            width = tile_width(tile)
            turn_ref[pl.ds((tile + 1) * PERIOD, PERIOD), pl.ds(0, width)] = out_grad[:, pl.ds(tile * LANES, width)]
        lane = lax.broadcasted_iota(jnp.int32, (TURN_TILES, LANES), 1)
        row = lax.broadcasted_iota(jnp.int32, (TURN_TILES, LANES), 0)
        for i in range(PERIOD):
            group, shift = divmod(SENONES * i, LANES)
            value = turn_ref[pl.ds(PERIOD + i, TURN_TILES, stride=PERIOD), :]
            at = pl.ds(base + group, TURN_TILES)
            if shift:
                before = turn_ref[pl.ds(i, TURN_TILES, stride=PERIOD), :]
                value = pltpu.roll(jnp.where(lane < LANES - shift, value, before), shift, 1)
                value = jnp.where((row == 0) & (lane < shift), flat_ref[at, :], value)
            flat_ref[at, :] = value

    second = head + body
    lane_row = lax.broadcasted_iota(jnp.int32, (8, LANES), 0)

    @pl.when(step == second)
    def _():
        sum_ref[...] = jnp.zeros_like(sum_ref)

    @pl.when((step >= second) & (step < second + chunks))
    def _():
        index = step - second
        first = index * chunk // shard
        start = margin + per_row * chunk * index
        totals = [[jnp.zeros((8, LANES), jnp.float32) for _ in range(per_row)] for _ in range(overlap)]
        for i in range(chunk // 8):
            rows = lane_row + (index * chunk + 8 * i)
            inside = [
                (rows >= (first + j) * shard) & (rows < (first + j + 1) * shard) for j in range(overlap)
            ]
            for tile in range(per_row):
                at = pl.ds(start + per_row * 8 * i + tile, 8, stride=per_row)
                rest = residual_ref[pl.ds(8 * i, 8), pl.ds(tile * LANES, LANES)]
                value = flat_ref[at, :] + rest
                flat_ref[at, :] = value
                signed = jnp.where(rest >= 0, value, -value)
                for j in range(overlap):
                    totals[j][tile] = totals[j][tile] + jnp.where(inside[j], signed, 0.0)
        for j in range(overlap):

            @pl.when(first + j < count)
            def _():
                at = pl.ds(pl.multiple_of((first + j) * 8, 8), 8)
                for tile in range(per_row):
                    columns = pl.ds(tile * LANES, LANES)
                    sum_ref[at, columns] = sum_ref[at, columns] + totals[j][tile]

    third = second + chunks

    @pl.when(step == third)
    def _():
        for block in range(count):
            total = jnp.sum(sum_ref[pl.ds(8 * block, 8), :], axis=0, keepdims=True)
            mean = total / shard
            sum_ref[pl.ds(8 * block, 8), :] = jnp.broadcast_to(mean, (8, mean.shape[1]))
            scale_ref[pl.ds(block, 1), :] = mean

    @pl.when(step >= third)
    def _():
        index = step - third
        first = index * chunk // shard
        start = margin + per_row * chunk * index
        scales = []
        for j in range(overlap):
            at = pl.ds(pl.multiple_of(jnp.minimum(first + j, count - 1) * 8, 8), 8)
            scales.append([sum_ref[at, pl.ds(tile * LANES, LANES)] for tile in range(per_row)])
        for i in range(chunk // 8):
            rows = lane_row + (index * chunk + 8 * i)
            for tile in range(per_row):
                scale = scales[0][tile]
                for j in range(1, overlap):
                    scale = jnp.where(rows >= (first + j) * shard, scales[j][tile], scale)
                at = pl.ds(start + per_row * 8 * i + tile, 8, stride=per_row)
                columns = pl.ds(tile * LANES, LANES)
                rest = residual_ref[pl.ds(8 * i, 8), columns]
                coded = jnp.where(rest >= 0, scale, -scale)
                new_ref[pl.ds(8 * i, 8), columns] = flat_ref[at, :] - coded


def code(grads, offset, residual, shard, margin):
    quarter, width = residual.shape
    count = quarter // shard
    tiles = quarter // 8
    chunk = 8 * max(f for f in range(1, 65) if tiles % f == 0)
    chunks = quarter // chunk
    overlap = (chunk - 1 + shard - 1) // shard + 1
    body = grads[-1].shape[0] // PERIOD
    split = grads[0].shape[0] // BLOCK if len(grads) > 1 else 0
    head = split + (grads[1].shape[0] // BLOCK if len(grads) > 1 else 0)
    third = head + body + chunks
    plan = dict(
        inputs=len(grads), head=head, split=split, body=body, chunk=chunk, chunks=chunks,
        shard=shard, margin=margin, overlap=overlap,
    )
    groups = margin + quarter * width // LANES

    def residual_map(s, _):
        return (jnp.where(s >= third, s - third, jnp.clip(s - head - body, 0, chunks - 1)), 0)

    specs = []
    if head:
        specs.append(pl.BlockSpec((BLOCK, UNITS), lambda s, _: (jnp.minimum(s, split - 1), 0)))
        specs.append(pl.BlockSpec((BLOCK, UNITS), lambda s, _: (jnp.clip(s - split, 0, head - split - 1), 0)))
    specs.append(pl.BlockSpec((PERIOD, SENONES), lambda s, _: (jnp.clip(s - head, 0, body - 1), 0)))
    specs.append(pl.BlockSpec((chunk, width), residual_map))
    return pl.pallas_call(
        functools.partial(code_kernel, plan),
        out_shape=(
            jax.ShapeDtypeStruct(residual.shape, jnp.float32),
            jax.ShapeDtypeStruct((count, width), jnp.float32),
        ),
        grid_spec=pltpu.PrefetchScalarGridSpec(
            num_scalar_prefetch=1,
            grid=(third + chunks,),
            in_specs=specs,
            out_specs=(
                pl.BlockSpec((chunk, width), lambda s, _: (jnp.maximum(s - third, 0), 0)),
                pl.BlockSpec((count, width), lambda s, _: (0, 0)),
            ),
            scratch_shapes=[
                pltpu.VMEM((groups + 3 * PERIOD_GROUPS, LANES), jnp.float32),
                pltpu.VMEM(((TURN_TILES + 1) * PERIOD, LANES), jnp.float32),
                pltpu.VMEM((8 * count, width), jnp.float32),
            ],
        ),
    )(offset, *grads, residual)


def body(
    feats,
    utt_lengths,
    frame_mask,
    targets,
    val_feats,
    val_mask,
    val_targets,
    master,
    first_moment,
    second_moment,
    residual,
    average,
):
    width = master.shape[1]
    shard_rows = master.shape[0]
    quarter_rows = residual.shape[0]
    wide_count = lax.axis_size("wide")
    node_count = lax.axis_size("node")
    node_at = lax.axis_index("node")
    wide_at = lax.axis_index("wide")
    params = unpack(gather_flat(master))
    w_in, b_in, w_mid, b_mid, w_out, b_out = params
    words = pack_signs(residual)
    all_words = lax.all_gather(words, "wide", axis=0, tiled=True).reshape(
        wide_count, quarter_rows, width // 32
    )
    own_words = lax.dynamic_slice_in_dim(all_words, wide_at * shard_rows, shard_rows, 1)
    stacked = lax.all_gather(stack_frames(feats, utt_lengths[0]), "node", axis=0, tiled=True)
    marks = lax.all_gather(jnp.stack([targets, frame_mask]), "node", axis=1, tiled=True)
    labels = marks[0]
    weights = marks[1].astype(jnp.float32)
    sig_one, h_one, sig_two, h_two, logits = run_layers(params, stacked)
    loss_part, lse, hit = frame_terms(logits, labels, weights)
    probs = jnp.exp(logits - lse[:, None])
    delta_out = (weights[:, None] * jnp.where(hit, probs - 1.0, probs)).astype(jnp.bfloat16)

    row_groups = width // LANES
    quarter_groups = quarter_rows * row_groups
    starts = []
    offsets = []
    lengths = []
    for node in range(node_count):
        begin = node * quarter_groups - HEAD_GROUPS
        start = max(begin, 0) * LANES // SENONES // PERIOD * PERIOD
        stop = -(-(begin + quarter_groups) * LANES // SENONES)
        starts.append(start)
        lengths.append(-(-(stop - start) // PERIOD) * PERIOD)
        offsets.append(start * SENONES // LANES - begin)
    margin = PERIOD_GROUPS + 5

    def first_quarter(_):
        back_two = contract_columns(delta_out, w_out)
        delta_two = (back_two * (sig_two * (1.0 - sig_two))).astype(jnp.bfloat16)
        back_one = contract_columns(delta_two, w_mid)
        delta_one = (back_one * (sig_one * (1.0 - sig_one))).astype(jnp.bfloat16)
        g_in = contract_rows(padded(stacked, -(-(D_IN + 1) // BLOCK) * BLOCK), delta_one)
        g_mid = contract_rows(padded(h_one, -(-(UNITS + 1) // BLOCK) * BLOCK), delta_two)
        g_out = contract_rows(h_two[:, : lengths[0]], delta_out)
        offset = jnp.full((1,), offsets[0], jnp.int32)
        return code((g_in, g_mid, g_out), offset, residual, shard_rows, 0)

    def other_quarter(_):
        span = max(lengths[1:])
        begin = jnp.asarray(starts, jnp.int32)[node_at]
        offset = jnp.asarray(offsets, jnp.int32)[node_at] + margin
        longest = max(start + span for start in starts)
        extended = padded(h_two, -(-longest // LANES) * LANES)
        picked = lax.dynamic_slice_in_dim(extended, begin, span, 1)
        g_out = contract_rows(picked, delta_out)
        return code((g_out,), offset[None], residual, shard_rows, margin)

    residual_new, scales = lax.cond(node_at == 0, first_quarter, other_quarter, 0)
    loss_sum, count = lax.psum((loss_part, jnp.sum(weights)), "wide")
    all_scales = lax.all_gather(scales, "wide", axis=0, tiled=True).reshape(
        wide_count, wide_count, width
    )
    own_scales = lax.dynamic_index_in_dim(all_scales, wide_at, 1, keepdims=False)
    decoded = jnp.sum(unpack_signs(own_words) * own_scales[:, None, :], axis=0)
    square_part = jnp.sum(decoded * decoded)
    square_sum = lax.psum(square_part, ("node", "wide"))
    grad_norm = jnp.sqrt(square_sum) / count
    factor = jnp.minimum(1.0, CLIP_NORM / (grad_norm + 1e-06))
    grad = decoded * (factor / count)
    first_new = BETA_ONE * first_moment + (1.0 - BETA_ONE) * grad
    second_new = BETA_TWO * second_moment + (1.0 - BETA_TWO) * grad * grad
    first_hat = first_new / (1.0 - BETA_ONE**STEP_COUNT)
    second_hat = second_new / (1.0 - BETA_TWO**STEP_COUNT)
    master_new = master - LEARN_RATE * (
        first_hat / (jnp.sqrt(second_hat) + EPS_ADAM) + DECAY * master
    )
    average_new = AVG_KEEP * average + (1.0 - AVG_KEEP) * master_new
    val_params = unpack(gather_flat(average_new))
    val_stacked = stack_frames(val_feats, jnp.full((1,), val_feats.shape[0], jnp.int32))
    val_logits = run_layers(val_params, val_stacked)[4]
    val_weights = val_mask.astype(jnp.float32)
    val_part = frame_terms(val_logits, val_targets, val_weights)[0]
    val_sum, val_count = lax.psum((val_part, jnp.sum(val_weights)), ("node", "wide"))
    return (
        loss_sum / count,
        val_sum / val_count,
        grad_norm,
        master_new,
        first_new,
        second_new,
        residual_new,
        average_new,
    )


def solution(mesh):
    return jax.shard_map(
        body,
        mesh=mesh,
        in_specs=(
            P(("node", "wide"), None),
            P(("node", "wide"), None),
            P(("node", "wide")),
            P(("node", "wide")),
            P(("node", "wide"), None),
            P(("node", "wide")),
            P(("node", "wide")),
            P(("node", "wide"), None),
            P(("node", "wide"), None),
            P(("node", "wide"), None),
            P(("node", "wide"), None),
            P(("node", "wide"), None),
        ),
        out_specs=(
            P(),
            P(),
            P(),
            P(("node", "wide"), None),
            P(("node", "wide"), None),
            P(("node", "wide"), None),
            P(("node", "wide"), None),
            P(("node", "wide"), None),
        ),
        check_vma=False,
    )
```

```python
import functools

import jax
import jax.numpy as jnp
from jax import lax
from jax.experimental import pallas as pl
from jax.experimental.pallas import tpu as pltpu
from jax.sharding import PartitionSpec as P

CONTEXT = 11
UNITS = 2048
SENONES = 9304
D_IN = 440
STEP_COUNT = 8
LANES = 128
PERIOD = 16
PERIOD_GROUPS = PERIOD * SENONES // LANES
TILES = -(-SENONES // LANES)
HEAD_ROWS = D_IN + 1 + UNITS + 1
HEAD_GROUPS = HEAD_ROWS * UNITS // LANES
TURN_TILES = 80
BLOCK = 104

CLIP_NORM = 1.0
LEARN_RATE = 0.02
BETA_ONE = 0.5
BETA_TWO = 0.5
DECAY = 0.1
AVG_KEEP = 0.9
EPS_ADAM = 1e-08


def stack_frames(feats, lengths):
    count = feats.shape[0]
    ends = jnp.cumsum(lengths)
    starts = ends - lengths
    where_t = jnp.arange(count, dtype=jnp.int32)[:, None]
    inside = (where_t >= starts[None, :]) & (where_t < ends[None, :])
    first = jnp.sum(jnp.where(inside, starts[None, :], 0), axis=1)
    last = jnp.sum(jnp.where(inside, ends[None, :], 0), axis=1) - 1
    offsets = jnp.arange(CONTEXT, dtype=jnp.int32) - CONTEXT // 2
    index = jnp.clip(where_t + offsets[None, :], first[:, None], last[:, None])
    return feats[index].reshape(count, CONTEXT * feats.shape[1])


def tile_width(tile):
    return min(LANES, SENONES - tile * LANES)


def window_of(step, plan):
    base = jnp.where(
        step == 0,
        0,
        jnp.where(
            step <= plan["middle"],
            plan["middle_at"] + plan["middle_span"] * (step - 1),
            HEAD_GROUPS + PERIOD * PERIOD_GROUPS * (step - 1 - plan["middle"]),
        ),
    )
    place = base + (plan["padded"] - plan["groups"]) * (base // plan["groups"])
    return base, jnp.minimum(place // plan["chunk"], plan["last"])


def unfold_kernel(plan, flat_ref, in_ref, mid_ref, out_ref, wide_ref, turn_ref):
    step_at = pl.program_id(0)
    chunk, margin = plan["chunk"], plan["margin"]
    base, window = window_of(step_at, plan)
    shift_by = plan["padded"] - plan["groups"]

    def widen(step, carry):
        place = (window + step) * chunk
        at = place - shift_by * (place // plan["padded"]) - base + margin
        source = pl.multiple_of(step * chunk, PERIOD)
        wide_ref[pl.ds(at, chunk), :] = flat_ref[pl.ds(source, chunk), :].astype(jnp.float32)
        return carry

    lax.fori_loop(0, plan["window"] // chunk, widen, 0)
    lane = lax.broadcasted_iota(jnp.int32, (TURN_TILES, LANES), 1)

    def straight(ref):
        tiles = UNITS // LANES

        def rows16(step, carry):
            rows = pl.ds(pl.multiple_of(step * PERIOD, PERIOD), PERIOD)
            for tile in range(tiles):
                at = margin + step * (PERIOD * tiles) + tile
                piece = wide_ref[pl.ds(at, PERIOD, stride=tiles), :]
                ref[rows, pl.ds(tile * LANES, LANES)] = piece.astype(jnp.bfloat16)
            return carry

        lax.fori_loop(0, ref.shape[0] // PERIOD, rows16, 0)

    def period(step, carry):
        start = margin + step * PERIOD_GROUPS
        for i in range(PERIOD):
            group, shift = divmod(SENONES * i, LANES)
            value = wide_ref[pl.ds(start + group, TURN_TILES), :]
            if shift:
                following = wide_ref[pl.ds(start + group + 1, TURN_TILES), :]
                value = pltpu.roll(jnp.where(lane >= shift, value, following), LANES - shift, 1)
            turn_ref[pl.ds(i, TURN_TILES, stride=PERIOD), :] = value
        rows = pl.ds(pl.multiple_of(step * PERIOD, PERIOD), PERIOD)
        for tile in range(TILES):
            width = tile_width(tile)
            piece = turn_ref[pl.ds(tile * PERIOD, PERIOD), :].astype(jnp.bfloat16)
            out_ref[rows, pl.ds(tile * LANES, width)] = piece[:, :width]
        return carry

    @pl.when(step_at == 0)
    def _():
        straight(in_ref)

    @pl.when((step_at > 0) & (step_at <= plan["middle"]))
    def _():
        straight(mid_ref)

    @pl.when(step_at > plan["middle"])
    def _():
        lax.fori_loop(0, out_ref.shape[0] // PERIOD, period, 0)


def unfold(flat, groups, padded):
    total = flat.shape[0]
    span = PERIOD * PERIOD
    needed = PERIOD * PERIOD_GROUPS
    middle = 2
    in_rows = -(-(D_IN + 1) // PERIOD) * PERIOD
    units = padded // PERIOD
    chunk = PERIOD * max(f for f in range(1, 51) if units % f == 0)
    crossed = -(-needed // groups) + 1
    window = chunk * (-(-(needed + crossed * (padded - groups) + TURN_TILES) // chunk) + 1)
    plan = dict(
        groups=groups,
        padded=padded,
        chunk=chunk,
        window=window,
        last=(total - window) // chunk,
        margin=window - needed + 2 * chunk,
        middle=middle,
        middle_at=(D_IN + 1) * UNITS // LANES,
        middle_span=UNITS // middle * UNITS // LANES,
    )

    def middle_map(s):
        return (jnp.clip(s - 1, 0, middle - 1), 0)

    return pl.pallas_call(
        functools.partial(unfold_kernel, plan),
        grid=(1 + middle + UNITS // span,),
        out_shape=(
            jax.ShapeDtypeStruct((in_rows, UNITS), jnp.bfloat16),
            jax.ShapeDtypeStruct((UNITS, UNITS), jnp.bfloat16),
            jax.ShapeDtypeStruct((UNITS, SENONES), jnp.bfloat16),
        ),
        in_specs=[
            pl.BlockSpec(
                (pl.Element(window), pl.Element(LANES)), lambda s: (chunk * window_of(s, plan)[1], 0)
            )
        ],
        out_specs=(
            pl.BlockSpec((in_rows, UNITS), lambda s: (0, 0)),
            pl.BlockSpec((UNITS // middle, UNITS), middle_map),
            pl.BlockSpec((span, SENONES), lambda s: (jnp.maximum(s - 1 - middle, 0), 0)),
        ),
        scratch_shapes=[
            pltpu.VMEM((plan["margin"] + window + chunk, LANES), jnp.float32),
            pltpu.VMEM((TURN_TILES * PERIOD, LANES), jnp.float32),
        ],
    )(flat)


def flat_slice(flat, groups, padded, begin, count):
    pieces = []
    while count:
        shard, inside = divmod(begin, groups)
        taken = min(count, groups - inside)
        pieces.append(flat[shard * padded + inside : shard * padded + inside + taken].reshape(-1))
        begin, count = begin + taken, count - taken
    return jnp.concatenate(pieces) if len(pieces) > 1 else pieces[0]


def low_flat(block):
    groups = block.shape[0] * block.shape[1] // LANES
    low = block.astype(jnp.bfloat16).reshape(groups, LANES)
    return jnp.pad(low, ((0, -groups % PERIOD), (0, 0)))


def gather_params(low, groups):
    padded = low.shape[0]
    flat = lax.all_gather(low, ("node", "wide"), axis=0, tiled=True)
    w_in, w_mid, w_out = unfold(flat, groups, padded)
    per_row = UNITS // LANES
    b_in = flat_slice(flat, groups, padded, D_IN * per_row, per_row)
    b_mid = flat_slice(flat, groups, padded, HEAD_GROUPS - per_row, per_row)
    b_out = flat_slice(flat, groups, padded, HEAD_GROUPS + UNITS * SENONES // LANES, TILES)[:SENONES]
    return (w_in[:D_IN], b_in, w_mid, b_mid, w_out, b_out), flat


def layer_forward(inputs, weight, bias):
    return jnp.dot(inputs, weight, preferred_element_type=jnp.float32) + bias.astype(jnp.float32)


def contract_rows(left, right):
    return lax.dot_general(left, right, (((0,), (0,)), ((), ())), preferred_element_type=jnp.float32)


def contract_columns(left, right):
    return lax.dot_general(left, right, (((1,), (1,)), ((), ())), preferred_element_type=jnp.float32)


def run_layers(params, stacked):
    w_in, b_in, w_mid, b_mid, w_out, b_out = params
    sig_one = jax.nn.sigmoid(layer_forward(stacked, w_in, b_in))
    h_one = sig_one.astype(jnp.bfloat16)
    sig_two = jax.nn.sigmoid(layer_forward(h_one, w_mid, b_mid))
    h_two = sig_two.astype(jnp.bfloat16)
    logits = layer_forward(h_two, w_out, b_out)
    return (sig_one, h_one, sig_two, h_two, logits)


def frame_terms(logits, labels, weights):
    hit = labels[:, None] == lax.broadcasted_iota(jnp.int32, logits.shape, 1)
    top = jnp.max(logits, axis=1)
    total = jnp.sum(jnp.exp(logits - top[:, None]), axis=1)
    picked = jnp.sum(jnp.where(hit, logits, 0.0), axis=1)
    lse = jnp.log(total) + top
    return (jnp.sum(weights * (lse - picked)), lse, hit)


def pack_signs(rest):
    bits = (rest >= 0).astype(jnp.int32).reshape(rest.shape[0], rest.shape[1] // 32, 32)
    shifts = jnp.arange(32, dtype=jnp.int32)
    return jnp.sum(jnp.left_shift(bits, shifts), axis=2)


def unpack_signs(words):
    shifts = jnp.arange(32, dtype=jnp.int32)
    bits = jnp.bitwise_and(jnp.right_shift(words[..., None], shifts), 1)
    signs = (2 * bits - 1).astype(jnp.float32)
    return signs.reshape(words.shape[:-1] + (words.shape[-1] * 32,))


def padded(values, columns):
    count = values.shape[0]
    one = jnp.ones((count, 1), jnp.bfloat16)
    rest = jnp.zeros((count, columns - values.shape[1] - 1), jnp.bfloat16)
    return jnp.concatenate([values, one, rest], axis=1)


def code_kernel(plan, offset_ref, *refs):
    grad_refs = refs[: plan["inputs"]]
    residual_ref, new_ref, scale_ref, flat_ref, turn_ref, sum_ref = refs[plan["inputs"] :]
    step = pl.program_id(0)
    head, body, chunks = plan["head"], plan["body"], plan["chunks"]
    chunk, shard, margin, overlap = plan["chunk"], plan["shard"], plan["margin"], plan["overlap"]
    count = sum_ref.shape[0] // 8
    per_row = residual_ref.shape[1] // LANES
    if head:

        def place(ref, row):
            for tile in range(UNITS // LANES):
                at = row * (UNITS // LANES) + tile
                flat_ref[pl.ds(at, BLOCK, stride=UNITS // LANES), :] = ref[:, pl.ds(tile * LANES, LANES)]

        split = plan["split"]

        @pl.when(step < split)
        def _():
            place(grad_refs[0], step * BLOCK)

        @pl.when((step >= split) & (step < head))
        def _():
            place(grad_refs[1], D_IN + 1 + (step - split) * BLOCK)

    out_grad = grad_refs[-1]

    @pl.when((step >= head) & (step < head + body))
    def _():
        base = offset_ref[0] + (step - head) * PERIOD_GROUPS
        for tile in range(TILES):
            width = tile_width(tile)
            turn_ref[pl.ds((tile + 1) * PERIOD, PERIOD), pl.ds(0, width)] = out_grad[:, pl.ds(tile * LANES, width)]
        lane = lax.broadcasted_iota(jnp.int32, (TURN_TILES, LANES), 1)
        row = lax.broadcasted_iota(jnp.int32, (TURN_TILES, LANES), 0)
        for i in range(PERIOD):
            group, shift = divmod(SENONES * i, LANES)
            value = turn_ref[pl.ds(PERIOD + i, TURN_TILES, stride=PERIOD), :]
            at = pl.ds(base + group, TURN_TILES)
            if shift:
                before = turn_ref[pl.ds(i, TURN_TILES, stride=PERIOD), :]
                value = pltpu.roll(jnp.where(lane < LANES - shift, value, before), shift, 1)
                value = jnp.where((row == 0) & (lane < shift), flat_ref[at, :], value)
            flat_ref[at, :] = value

    second = head + body
    lane_row = lax.broadcasted_iota(jnp.int32, (8, LANES), 0)

    @pl.when(step == second)
    def _():
        sum_ref[...] = jnp.zeros_like(sum_ref)

    @pl.when((step >= second) & (step < second + chunks))
    def _():
        index = step - second
        first = index * chunk // shard
        start = margin + per_row * chunk * index
        totals = [[jnp.zeros((8, LANES), jnp.float32) for _ in range(per_row)] for _ in range(overlap)]
        for i in range(chunk // 8):
            rows = lane_row + (index * chunk + 8 * i)
            inside = [
                (rows >= (first + j) * shard) & (rows < (first + j + 1) * shard) for j in range(overlap)
            ]
            for tile in range(per_row):
                at = pl.ds(start + per_row * 8 * i + tile, 8, stride=per_row)
                rest = residual_ref[pl.ds(8 * i, 8), pl.ds(tile * LANES, LANES)]
                value = flat_ref[at, :] + rest
                flat_ref[at, :] = value
                signed = jnp.where(rest >= 0, value, -value)
                for j in range(overlap):
                    totals[j][tile] = totals[j][tile] + jnp.where(inside[j], signed, 0.0)
        for j in range(overlap):

            @pl.when(first + j < count)
            def _():
                at = pl.ds(pl.multiple_of((first + j) * 8, 8), 8)
                for tile in range(per_row):
                    columns = pl.ds(tile * LANES, LANES)
                    sum_ref[at, columns] = sum_ref[at, columns] + totals[j][tile]

    third = second + chunks

    @pl.when(step == third)
    def _():
        for block in range(count):
            total = jnp.sum(sum_ref[pl.ds(8 * block, 8), :], axis=0, keepdims=True)
            mean = total / shard
            sum_ref[pl.ds(8 * block, 8), :] = jnp.broadcast_to(mean, (8, mean.shape[1]))
            scale_ref[pl.ds(block, 1), :] = mean

    @pl.when(step >= third)
    def _():
        index = step - third
        first = index * chunk // shard
        start = margin + per_row * chunk * index
        scales = []
        for j in range(overlap):
            at = pl.ds(pl.multiple_of(jnp.minimum(first + j, count - 1) * 8, 8), 8)
            scales.append([sum_ref[at, pl.ds(tile * LANES, LANES)] for tile in range(per_row)])
        for i in range(chunk // 8):
            rows = lane_row + (index * chunk + 8 * i)
            for tile in range(per_row):
                scale = scales[0][tile]
                for j in range(1, overlap):
                    scale = jnp.where(rows >= (first + j) * shard, scales[j][tile], scale)
                at = pl.ds(start + per_row * 8 * i + tile, 8, stride=per_row)
                columns = pl.ds(tile * LANES, LANES)
                rest = residual_ref[pl.ds(8 * i, 8), columns]
                coded = jnp.where(rest >= 0, scale, -scale)
                new_ref[pl.ds(8 * i, 8), columns] = flat_ref[at, :] - coded


def code(grads, offset, residual, shard, margin):
    quarter, width = residual.shape
    count = quarter // shard
    tiles = quarter // 8
    chunk = 8 * max(f for f in range(1, 65) if tiles % f == 0)
    chunks = quarter // chunk
    overlap = (chunk - 1 + shard - 1) // shard + 1
    body = grads[-1].shape[0] // PERIOD
    split = grads[0].shape[0] // BLOCK if len(grads) > 1 else 0
    head = split + (grads[1].shape[0] // BLOCK if len(grads) > 1 else 0)
    third = head + body + chunks
    plan = dict(
        inputs=len(grads), head=head, split=split, body=body, chunk=chunk, chunks=chunks,
        shard=shard, margin=margin, overlap=overlap,
    )
    groups = margin + quarter * width // LANES

    def residual_map(s, _):
        return (jnp.where(s >= third, s - third, jnp.clip(s - head - body, 0, chunks - 1)), 0)

    specs = []
    if head:
        specs.append(pl.BlockSpec((BLOCK, UNITS), lambda s, _: (jnp.minimum(s, split - 1), 0)))
        specs.append(pl.BlockSpec((BLOCK, UNITS), lambda s, _: (jnp.clip(s - split, 0, head - split - 1), 0)))
    specs.append(pl.BlockSpec((PERIOD, SENONES), lambda s, _: (jnp.clip(s - head, 0, body - 1), 0)))
    specs.append(pl.BlockSpec((chunk, width), residual_map))
    return pl.pallas_call(
        functools.partial(code_kernel, plan),
        out_shape=(
            jax.ShapeDtypeStruct(residual.shape, jnp.float32),
            jax.ShapeDtypeStruct((count, width), jnp.float32),
        ),
        grid_spec=pltpu.PrefetchScalarGridSpec(
            num_scalar_prefetch=1,
            grid=(third + chunks,),
            in_specs=specs,
            out_specs=(
                pl.BlockSpec((chunk, width), lambda s, _: (jnp.maximum(s - third, 0), 0)),
                pl.BlockSpec((count, width), lambda s, _: (0, 0)),
            ),
            scratch_shapes=[
                pltpu.VMEM((groups + 3 * PERIOD_GROUPS, LANES), jnp.float32),
                pltpu.VMEM(((TURN_TILES + 1) * PERIOD, LANES), jnp.float32),
                pltpu.VMEM((8 * count, width), jnp.float32),
            ],
        ),
    )(offset, *grads, residual)


def body(
    feats,
    utt_lengths,
    frame_mask,
    targets,
    val_feats,
    val_mask,
    val_targets,
    master,
    first_moment,
    second_moment,
    residual,
    average,
):
    width = master.shape[1]
    shard_rows = master.shape[0]
    quarter_rows = residual.shape[0]
    wide_count = lax.axis_size("wide")
    node_count = lax.axis_size("node")
    node_at = lax.axis_index("node")
    wide_at = lax.axis_index("wide")
    groups = shard_rows * width // LANES
    low = low_flat(master)
    params, flat = gather_params(low, groups)
    w_in, b_in, w_mid, b_mid, w_out, b_out = params
    low, rest, feats, frame_mask, val_mask = lax.optimization_barrier((low, residual, feats, frame_mask, val_mask))
    stacked = lax.all_gather(stack_frames(feats, utt_lengths[0]), "node", axis=0, tiled=True)
    marks = lax.all_gather(jnp.stack([targets, frame_mask]), "node", axis=1, tiled=True)
    labels = marks[0]
    weights = marks[1].astype(jnp.float32)
    val_weights = val_mask.astype(jnp.float32)
    count, val_count = lax.psum((jnp.sum(frame_mask.astype(jnp.float32)), jnp.sum(val_weights)), ("node", "wide"))
    words, flat = lax.optimization_barrier((pack_signs(rest), flat))
    all_words = lax.all_gather(words, "wide", axis=0, tiled=True).reshape(
        wide_count, quarter_rows, width // 32
    )
    own_words = lax.dynamic_slice_in_dim(all_words, wide_at * shard_rows, shard_rows, 1)
    sig_one, h_one, sig_two, h_two, logits = run_layers(params, stacked)
    loss_part, lse, hit = frame_terms(logits, labels, weights)
    probs = jnp.exp(logits - lse[:, None])
    delta_out = (weights[:, None] * jnp.where(hit, probs - 1.0, probs)).astype(jnp.bfloat16)

    row_groups = width // LANES
    quarter_groups = quarter_rows * row_groups
    starts = []
    offsets = []
    lengths = []
    for node in range(node_count):
        begin = node * quarter_groups - HEAD_GROUPS
        start = max(begin, 0) * LANES // SENONES // PERIOD * PERIOD
        stop = -(-(begin + quarter_groups) * LANES // SENONES)
        starts.append(start)
        lengths.append(-(-(stop - start) // PERIOD) * PERIOD)
        offsets.append(start * SENONES // LANES - begin)
    margin = PERIOD_GROUPS + 5

    def first_quarter(_):
        back_two = contract_columns(delta_out, w_out)
        delta_two = (back_two * (sig_two * (1.0 - sig_two))).astype(jnp.bfloat16)
        back_one = contract_columns(delta_two, w_mid)
        delta_one = (back_one * (sig_one * (1.0 - sig_one))).astype(jnp.bfloat16)
        g_in = contract_rows(padded(stacked, -(-(D_IN + 1) // BLOCK) * BLOCK), delta_one)
        g_mid = contract_rows(padded(h_one, -(-(UNITS + 1) // BLOCK) * BLOCK), delta_two)
        g_out = contract_rows(h_two[:, : lengths[0]], delta_out)
        offset = jnp.full((1,), offsets[0], jnp.int32)
        return code((g_in, g_mid, g_out), offset, residual, shard_rows, 0)

    def other_quarter(_):
        span = max(lengths[1:])
        begin = jnp.asarray(starts, jnp.int32)[node_at]
        offset = jnp.asarray(offsets, jnp.int32)[node_at] + margin
        longest = max(start + span for start in starts)
        extended = padded(h_two, -(-longest // LANES) * LANES)
        picked = lax.dynamic_slice_in_dim(extended, begin, span, 1)
        g_out = contract_rows(picked, delta_out)
        return code((g_out,), offset[None], residual, shard_rows, margin)

    residual_new, scales = lax.cond(node_at == 0, first_quarter, other_quarter, 0)
    all_scales = lax.all_gather(scales, "wide", axis=0, tiled=True).reshape(
        wide_count, wide_count, width
    )
    own_scales = lax.dynamic_index_in_dim(all_scales, wide_at, 1, keepdims=False)
    decoded = jnp.sum(unpack_signs(own_words) * own_scales[:, None, :], axis=0)
    square_part = jnp.sum(decoded * decoded)
    square_sum = lax.psum(square_part, ("node", "wide"))
    grad_norm = jnp.sqrt(square_sum) / count
    factor = jnp.minimum(1.0, CLIP_NORM / (grad_norm + 1e-06))
    grad = decoded * (factor / count)
    first_new = BETA_ONE * first_moment + (1.0 - BETA_ONE) * grad
    second_new = BETA_TWO * second_moment + (1.0 - BETA_TWO) * grad * grad
    first_hat = first_new / (1.0 - BETA_ONE**STEP_COUNT)
    second_hat = second_new / (1.0 - BETA_TWO**STEP_COUNT)
    master_new = master - LEARN_RATE * (
        first_hat / (jnp.sqrt(second_hat) + EPS_ADAM) + DECAY * master
    )
    average_new = AVG_KEEP * average + (1.0 - AVG_KEEP) * master_new
    val_params, _ = gather_params(low_flat(average_new), groups)
    val_stacked = stack_frames(val_feats, jnp.full((1,), val_feats.shape[0], jnp.int32))
    val_logits = run_layers(val_params, val_stacked)[4]
    val_part = frame_terms(val_logits, val_targets, val_weights)[0]
    loss_own = jnp.where(node_at == 0, loss_part, 0.0)
    loss_sum, val_sum = lax.psum((loss_own, val_part), ("node", "wide"))
    return (
        loss_sum / count,
        val_sum / val_count,
        grad_norm,
        master_new,
        first_new,
        second_new,
        residual_new,
        average_new,
    )


def solution(mesh):
    return jax.shard_map(
        body,
        mesh=mesh,
        in_specs=(
            P(("node", "wide"), None),
            P(("node", "wide"), None),
            P(("node", "wide")),
            P(("node", "wide")),
            P(("node", "wide"), None),
            P(("node", "wide")),
            P(("node", "wide")),
            P(("node", "wide"), None),
            P(("node", "wide"), None),
            P(("node", "wide"), None),
            P(("node", "wide"), None),
            P(("node", "wide"), None),
        ),
        out_specs=(
            P(),
            P(),
            P(),
            P(("node", "wide"), None),
            P(("node", "wide"), None),
            P(("node", "wide"), None),
            P(("node", "wide"), None),
            P(("node", "wide"), None),
        ),
        check_vma=False,
    )
```
